32 devices in a mesh: dp: 16 (over z, y, x), mp: 2 (over core).
Axes of the slice: x: 2, y: 2, z: 4, core: 2. Of those that a mesh axis runs over, the one named last changes fastest.
Arguments:
- tokens: bfloat16 [16, 512, 768], P('dp'), may hold values from -6 to 6
- cotangent: float32 [16, 128, 768], P('dp'), may hold values from -6 to 6
- masked_pos: int32 [16, 128], P('dp'), may hold values from -1 to 511, as said below
- w_qkv: bfloat16 [3, 768, 768], P(None, None, 'mp'), may hold values from -0.21875 to 0.21875
- b_qkv: float32 [3, 768], P(None, 'mp'), may hold values from -3 to 3
- w_out: bfloat16 [768, 768], P('mp'), may hold values from -0.625 to 0.625
- b_out: float32 [768], replicated, may hold values from -3 to 3
- w_in: bfloat16 [768, 3072], P(None, 'mp'), may hold values from -0.21875 to 0.21875
- b_in: float32 [3072], P('mp'), may hold values from -3 to 3
- w_back: bfloat16 [3072, 768], P('mp'), may hold values from -0.109375 to 0.109375
- b_back: float32 [768], replicated, may hold values from -3 to 3
- ln_gain: float32 [2, 768], replicated, may hold values from 0.5 to 1.5
- ln_bias: float32 [2, 768], replicated, may hold values from -2 to 2
Outputs:
- output: bfloat16 [16, 512, 768], P('dp')
- grad_tokens: float32 [16, 512, 768], P('dp')
- grad_w_qkv: float32 [3, 768, 768], P(None, 'dp', 'mp')
- grad_b_qkv: float32 [3, 768], P(None, 'mp')
- grad_w_out: float32 [768, 768], P('mp', 'dp')
- grad_b_out: float32 [768], replicated
- grad_w_in: float32 [768, 3072], P('dp', 'mp')
- grad_b_in: float32 [3072], P('mp')
- grad_w_back: float32 [3072, 768], P('mp', 'dp')
- grad_b_back: float32 [768], replicated
- grad_ln_gain: float32 [2, 768], replicated
- grad_ln_bias: float32 [2, 768], replicated
The draws below stay inside these ranges and needn't reach their ends.
Inputs may be any that keep to these rules, and one draw needn't show every extreme that they name: `masked_pos`: each row lists between 25 and 128 distinct positions in increasing order, then -1 in the remaining slots; some row lists exactly 128.
All inputs are finite; a program needn't handle non-finite values.
Results may differ from the reference program's by a relative error of at most 0.014.
Values sent between devices are 32-bit elements; how exact they have to be, the bound alone decides.
No kernel may reach another device: no remote copies, remote signals or barrier semaphores. Data moves between devices by JAX's collectives and lax.ppermute only.
A program may use at most 128 MiB of HBM per device.

```python
import jax
import jax.numpy as jnp
from jax import lax

D = 768
HEADS = 12
HEAD_DIM = 64
FF = 3072
L = 512
MASK_MAX = 128
SEQS = 16


def draw_masked_pos(key, part):
    count_key = jax.random.fold_in(key, 11)
    order_key = jax.random.fold_in(key, 12)
    pick_key = jax.random.fold_in(key, 13)
    lowest = max(1, L // 20)
    counts = jax.random.randint(count_key, (SEQS,), lowest, MASK_MAX + 1)
    chosen = jax.random.randint(pick_key, (), 0, SEQS)
    counts = jnp.where(jnp.arange(SEQS) == chosen, MASK_MAX, counts)
    row_keys = jax.random.split(order_key, SEQS)
    orders = jax.vmap(lambda k: jax.random.permutation(k, L))(row_keys)[:, :MASK_MAX]
    slot = jnp.arange(MASK_MAX)[None, :]
    picked = jnp.where(slot < counts[:, None], orders, L)
    picked = jnp.sort(picked, axis=1)
    return jnp.where(picked < L, picked, -1).astype(jnp.int32)


def strengthened(drawn, key, source, target, shards_of, factor):
    def block_of(axis_at):
        return (jnp.arange(drawn.shape[axis_at]) // (drawn.shape[axis_at] // shards_of)).reshape((-1,) + (1,) * (drawn.ndim - 1 - axis_at))

    first = jax.random.permutation(key, shards_of)[block_of(target)]
    second = (block_of(target) + shards_of // 2) % shards_of
    return jnp.where((block_of(source) == first) | (block_of(source) == second), factor * drawn, drawn)


def block_levels(own_key, dims, pieces, low, top_value):
    def one(position, shards_of):
        steps = jax.random.uniform(jax.random.fold_in(jax.random.fold_in(own_key, 6), position), (shards_of,), jnp.float32, low / len(pieces), top_value / len(pieces))
        return jnp.repeat(jnp.exp(steps), dims[position] // shards_of).reshape((-1,) + (1,) * (len(dims) - position - 1))

    factor_of = one(*pieces[0])
    for cut in pieces[1:]:
        factor_of = factor_of * one(*cut)
    return factor_of


def centred(key, extent, scale, most, cuts=(), dtype=jnp.bfloat16):
    values = scale * jax.random.normal(key, extent, jnp.float32)
    if cuts:
        values = values * block_levels(key, extent, cuts, -0.22, 0.18)
    return jnp.clip(values, -most, most).astype(dtype)


def bell_draw_with(key, dims, scale, limit, cuts, heavy, kind=jnp.bfloat16):
    drawn = scale * jax.random.normal(key, dims, jnp.float32)
    if cuts:
        drawn = drawn * block_levels(key, dims, cuts, -0.22, 0.18)
    return jnp.clip(strengthened(drawn, jax.random.fold_in(key, 3), *heavy), -limit, limit).astype(kind)


def setup_inputs(seed: int = 0) -> dict:
    key_list = jax.random.split(jax.random.key(seed), 14)
    tokens = centred(key_list[0], (SEQS, L, D), 1.0, 6.0, ((0, 16),))
    cotangent = bell_draw_with(key_list[1], (SEQS, MASK_MAX, D), 1.0, 6.0, ((0, 16),), (0, 2, 16, 2.0), jnp.float32)
    masked_pos = draw_masked_pos(jax.random.fold_in(key_list[13], 71), 0)
    w_qkv = centred(key_list[3], (3, D, D), D ** -0.5, 0.21875, ((2, 2),))
    b_qkv = centred(key_list[4], (3, D), 0.5, 3.0, ((1, 2),), jnp.float32)
    w_out = centred(key_list[5], (D, D), (D // 8) ** -0.5, 0.625, ((0, 2),))
    b_out = centred(key_list[6], (D,), 0.5, 3.0, (), jnp.float32)
    w_in = centred(key_list[7], (D, FF), D ** -0.5, 0.21875, ((1, 2),))
    b_in = centred(key_list[8], (FF,), 0.5, 3.0, ((0, 2),), jnp.float32)
    w_back = centred(key_list[9], (FF, D), FF ** -0.5, 0.109375, ((0, 2),))
    b_back = centred(key_list[10], (D,), 0.5, 3.0, (), jnp.float32)
    ln_gain = jnp.clip(1.0 + 0.1 * jax.random.normal(key_list[11], (2, D), jnp.float32), 0.5, 1.5)
    ln_bias = centred(key_list[12], (2, D), 0.3, 2.0, (), jnp.float32)
    return dict(tokens=tokens, cotangent=cotangent, masked_pos=masked_pos, w_qkv=w_qkv, b_qkv=b_qkv, w_out=w_out, b_out=b_out, w_in=w_in, b_in=b_in, w_back=w_back, b_back=b_back, ln_gain=ln_gain, ln_bias=ln_bias)


@jax.custom_vjp
def low(v):
    return lax.optimization_barrier(v.astype(jnp.bfloat16)).astype(jnp.float32)

@jax.custom_vjp
def low_back(v):
    return v

def low_keep(v):
    return (low(v), None)

def low_pass(kept, grad):
    return (grad,)

def back_keep(v):
    return (v, None)

def back_low(kept, grad):
    return (low(grad),)
low.defvjp(low_keep, low_pass)
low_back.defvjp(back_keep, back_low)
EPS = 1e-06
HIGH = lax.Precision.HIGHEST

def layer_norm(value, gain, shift):
    center = value - lax.optimization_barrier(jnp.mean(value, -1, keepdims=True))
    spread = lax.optimization_barrier(jnp.mean(center * center, -1, keepdims=True))
    return center * lax.rsqrt(spread + EPS) * gain + shift

def rotary_tables(length, half):
    place = jnp.arange(length).astype(jnp.float32)[:, None]
    freq = 10000.0 ** (-jnp.arange(half).astype(jnp.float32) / half)
    angle = place * freq
    return (jnp.cos(angle), jnp.sin(angle))

def rotate(value, cosine, sine):
    half = value.shape[-1] // 2
    first = value[..., :half]
    second = value[..., half:]
    return jnp.concatenate([first * cosine - second * sine, second * cosine + first * sine], -1)

def forward(tokens, w_qkv, b_qkv, w_out, b_out, w_in, b_in, w_back, b_back, ln_gain, ln_bias):
    group, length, width = tokens.shape
    cosine, sine = rotary_tables(length, HEAD_DIM // 2)
    cosine = cosine[None, :, None, :]
    sine = sine[None, :, None, :]
    pre = jnp.einsum('gld,jde->jgle', tokens, w_qkv, precision=HIGH) + b_qkv[:, None, None, :]
    pre = low_back(pre)

    def heads_of(value):
        return value.reshape(group, length, HEADS, HEAD_DIM)
    query = low(rotate(heads_of(pre[0]), cosine, sine))
    keys = low(rotate(heads_of(pre[1]), cosine, sine))
    values = low(heads_of(pre[2]))
    scores = low_back(jnp.einsum('gqhe,gkhe->ghqk', query, keys, precision=HIGH) * HEAD_DIM ** (-0.5))
    prob = low(jax.nn.softmax(scores, axis=-1))
    context = jnp.einsum('ghqk,gkhe->gqhe', prob, values, precision=HIGH)
    context = low(low_back(context)).reshape(group, length, width)
    attn = low_back(jnp.matmul(context, w_out, precision=HIGH) + b_out)
    h_one = layer_norm(tokens + attn, ln_gain[0], ln_bias[0])
    hidden = low_back(jnp.matmul(low(h_one), w_in, precision=HIGH) + b_in)
    act = low(jax.nn.gelu(hidden, approximate=False))
    ffn = low_back(jnp.matmul(act, w_back, precision=HIGH) + b_back)
    return layer_norm(h_one + ffn, ln_gain[1], ln_bias[1])

def reference(tokens, cotangent, masked_pos, w_qkv, b_qkv, w_out, b_out, w_in, b_in, w_back, b_back, ln_gain, ln_bias):
    params = tuple((p.astype(jnp.float32) for p in (w_qkv, b_qkv, w_out, b_out, w_in, b_in, w_back, b_back, ln_gain, ln_bias)))
    group = 8
    count = tokens.shape[0] // group
    tok_groups = tokens.reshape(count, group, L, D)
    cot_groups = cotangent.reshape(count, group, MASK_MAX, D)
    pos_groups = masked_pos.reshape(count, group, MASK_MAX)
    seq_index = jnp.arange(group).astype(jnp.int32)[:, None]

    def one_group(carry, items):
        tok_group, cot_group, pos_group = items
        result, pull = jax.vjp(forward, tok_group.astype(jnp.float32), *params)
        target = jnp.where(pos_group >= 0, pos_group, L).astype(jnp.int32)
        dense = jnp.zeros((group, L, D), jnp.float32).at[seq_index, target].add(cot_group.astype(jnp.float32), mode='drop')
        grads = pull(dense)
        carry = tuple((c + g for c, g in zip(carry, grads[1:])))
        return (carry, (result.astype(jnp.bfloat16), grads[0]))
    start = tuple((jnp.zeros(p.shape, jnp.float32) for p in params))
    sums, (outs, grad_tok) = lax.scan(one_group, start, (tok_groups, cot_groups, pos_groups))
    output = outs.reshape(tokens.shape)
    grad_tokens = grad_tok.reshape(tokens.shape)
    return (output, grad_tokens, sums[0], sums[1], sums[2], sums[3], sums[4], sums[5], sums[6], sums[7], sums[8], sums[9])
```

```python
import jax
import jax.numpy as jnp
import numpy as np
from jax import lax
from jax.experimental import pallas as pl
from jax.experimental.pallas import tpu as pltpu
from jax.sharding import PartitionSpec as P

HEAD_DIM = 64
PAIR = 2 * HEAD_DIM
EPS = 1e-06
F32 = jnp.float32
LOW = jnp.bfloat16


def tables(length):
    half = HEAD_DIM // 2
    freq = np.float32(10000.0) ** (-np.arange(half).astype(np.float32) / np.float32(half))
    angle = np.arange(length).astype(np.float32)[:, None] * freq.astype(np.float32)
    cosine = np.cos(angle).astype(np.float32)
    sine = np.sin(angle).astype(np.float32)
    cos_pair = np.concatenate([cosine] * 4, 1)
    sin_pair = np.concatenate([-sine, sine, -sine, sine], 1)
    return jnp.asarray(cos_pair), jnp.asarray(sin_pair)


def dot(left, right):
    return jnp.dot(left, right, preferred_element_type=F32)


def dot_nt(left, right):
    return lax.dot_general(left, right, (((1,), (1,)), ((), ())), preferred_element_type=F32)


def dot_tn(left, right):
    return lax.dot_general(left, right, (((0,), (0,)), ((), ())), preferred_element_type=F32)


def first_half(shape):
    return lax.broadcasted_iota(jnp.int32, shape, 1) % HEAD_DIM < HEAD_DIM // 2


def first_head(shape):
    return lax.broadcasted_iota(jnp.int32, shape, 1) < HEAD_DIM


def swapped(value):
    half = HEAD_DIM // 2
    ahead = pltpu.roll(value, PAIR - half, 1)
    behind = pltpu.roll(value, half, 1)
    return jnp.where(first_half(value.shape), ahead, behind)


def turn(value, cosine, sine):
    return value * cosine + swapped(value) * sine


def center_of(value):
    center = value - jnp.mean(value, -1, keepdims=True)
    scale = lax.rsqrt(jnp.mean(center * center, -1, keepdims=True) + EPS)
    return center * scale, scale


def norm_back(grad, hat, scale, gain):
    grad_hat = grad * gain
    mean_one = jnp.mean(grad_hat, -1, keepdims=True)
    mean_two = jnp.mean(grad_hat * hat, -1, keepdims=True)
    return scale * (grad_hat - mean_one - hat * mean_two)


def cdf_of(value):
    return 0.5 * (1.0 + lax.erf(value * np.float32(0.5**0.5)))


def gelu_slope(value, cdf):
    return cdf + value * (np.float32(1 / (2 * np.pi) ** 0.5) * jnp.exp(-0.5 * value * value))


def one_hot(pos_ref, length):
    pos = pos_ref[...]
    return lax.broadcasted_iota(jnp.int32, (pos.shape[0], length), 1) == pos


def col_sum(value):
    return jnp.sum(value, 0, keepdims=True)


def softmax_of(scores):
    expo = jnp.exp(scores - jnp.max(scores, -1, keepdims=True))
    return expo / jnp.sum(expo, -1, keepdims=True)


def front_kernel(
    tok, w_qkv, b_qkv, cos, sin, pos, w_out, q_o, k_o, v_o, qs_o, ts_o, cs_o, ss_o, prob_o, ctx_o, attn_o
):
    length = tok.shape[0]
    local = w_qkv.shape[2]
    pairs = local // PAIR
    hot_f = one_hot(pos, length).astype(F32)
    hot = hot_f.astype(LOW)
    rows = tok[...]
    ts_o[...] = dot(hot, rows).astype(LOW)
    cs_o[...] = jnp.dot(hot_f, cos[...], precision=lax.Precision.HIGHEST)
    ss_o[...] = jnp.dot(hot_f, sin[...], precision=lax.Precision.HIGHEST)
    pre_q = dot(rows, w_qkv[0]) + b_qkv[0:1, :]
    pre_k = dot(rows, w_qkv[1]) + b_qkv[1:2, :]
    v_o[...] = (dot(rows, w_qkv[2]) + b_qkv[2:3, :]).astype(LOW)
    for j in range(pairs):
        cut = slice(j * PAIR, (j + 1) * PAIR)
        q_o[:, cut] = turn(pre_q[:, cut], cos[...], sin[...]).astype(LOW)
        k_o[:, cut] = turn(pre_k[:, cut], cos[...], sin[...]).astype(LOW)
    qs_o[...] = dot(hot, q_o[...]).astype(LOW)
    for j in range(pairs):
        cut = slice(j * PAIR, (j + 1) * PAIR)
        query = qs_o[:, cut]
        keys = k_o[:, cut]
        values = v_o[:, cut]
        lead = first_head(query.shape)
        parts = []
        for side in range(2):
            chosen = jnp.where(lead if side == 0 else ~lead, query.astype(F32), 0.0).astype(LOW)
            prob = softmax_of(dot_nt(chosen, keys) * HEAD_DIM**-0.5)
            prob_o[2 * j + side] = prob
            parts.append(dot(prob.astype(LOW), values))
        ctx_o[:, cut] = jnp.where(lead, parts[0], parts[1]).astype(LOW)
    attn_o[...] = dot(ctx_o[...], w_out[...])


def mid_kernel(
    mpi, mine, other, tok, b_out, gain, shift, w_in, b_in, w_back, one_o, part_o, hat_o, scale_o, slope_o, half_o
):
    h_pre = tok[...].astype(F32) + (mine[...] + other[...] + b_out[...])
    hat, scale = center_of(h_pre)
    h_one = hat * gain[0:1, :] + shift[0:1, :]
    one_o[...] = h_one
    hidden = dot(h_one.astype(LOW), w_in[...]) + b_in[...]
    cdf = cdf_of(hidden)
    part_o[...] = dot((hidden * cdf).astype(LOW), w_back[...])
    hat_o[...] = hat
    scale_o[...] = scale
    slope_o[...] = gelu_slope(hidden, cdf)
    count = half_o.shape[0]
    half_o[...] = jnp.where(mpi[0] == 0, h_one[:count], h_one[count:])


def turn_kernel(
    mpi, mine, other, h_one, b_back, gain, cot, pos, slope, w_in, w_back, gz_o, half_o, part_o, small_o
):
    width = h_one.shape[1]
    z_sum = h_one[...] + (mine[...] + other[...] + b_back[...])
    hat, scale = center_of(z_sum)
    grad = jnp.where(pos[...] >= 0, cot[...], 0.0)
    grad_z = norm_back(grad, hat, scale, gain[1:2, :])
    gz_o[...] = grad_z
    count = half_o.shape[0]
    half_o[...] = jnp.where(mpi[0] == 0, grad_z[:count], grad_z[count:])
    grad_y = grad_z.astype(LOW)
    grad_u = (dot_nt(grad_y, w_back[...]) * slope[...]).astype(LOW)
    part_o[...] = dot_nt(grad_u, w_in[...])
    small_o[...] = jnp.zeros(small_o.shape, F32)
    small_o[0:1, :] = col_sum(grad_u.astype(F32))
    small_o[2:3, width:] = col_sum(grad_y.astype(F32))
    small_o[3:4, width:] = col_sum(grad * hat)
    small_o[4:5, width:] = col_sum(grad)


def back_kernel(
    place, mine, other, grad_z, hat, scale, gain, tok, tok_sel, ctx, w_out, q_sel, keys, values, prob, w_qkv,
    pos, cos, sin, cos_sel, sin_sel, small,
    dq_o, dk_o, dv_o, do_o, part_o, small_o, pre_o, gk_s, gv_s, gq_s,
):
    length, width = tok.shape
    local = w_out.shape[0]
    pairs = local // PAIR
    blocks = dq_o.shape[0]
    chunk = width // blocks
    grad_h = mine[...] + other[...] + grad_z[...]
    g_pre = norm_back(grad_h, hat[...], scale[...], gain[0:1, :])
    pre_o[...] = g_pre
    g_attn = g_pre.astype(LOW)
    small_o[...] = small[...]
    small_o[2:3, :width] = col_sum(g_attn.astype(F32))
    small_o[3:4, :width] = col_sum(grad_h * hat[...])
    small_o[4:5, :width] = col_sum(grad_h)

    def spread(out_ref, value, order):
        for c in range(blocks):
            out_ref[place[order, c]] = value[c * chunk : (c + 1) * chunk]

    spread(do_o, dot_tn(g_attn, ctx[...]), 0)
    g_ctx = dot_nt(g_attn, w_out[...]).astype(LOW)
    hot = one_hot(pos, length).astype(F32).astype(LOW)
    for j in range(pairs):
        cut = slice(j * PAIR, (j + 1) * PAIR)
        key_pair = keys[:, cut]
        value_pair = values[:, cut]
        query_pair = q_sel[:, cut].astype(F32)
        ctx_pair = g_ctx[:, cut].astype(F32)
        lead = first_head(query_pair.shape)
        g_q, g_k, g_v = [], None, None
        for side in range(2):
            keep = lead if side == 0 else ~lead
            q_one = jnp.where(keep, query_pair, 0.0).astype(LOW)
            c_one = jnp.where(keep, ctx_pair, 0.0).astype(LOW)
            weight = prob[2 * j + side]
            g_prob = dot_nt(c_one, value_pair)
            inner = jnp.sum(weight * g_prob, -1, keepdims=True)
            g_score = (weight * (g_prob - inner)).astype(LOW)
            add_v = dot_tn(weight.astype(LOW), c_one)
            add_k = dot_tn(g_score, q_one)
            g_v = add_v if g_v is None else g_v + add_v
            g_k = add_k if g_k is None else g_k + add_k
            g_q.append(dot(g_score, key_pair))
        g_q = jnp.where(lead, g_q[0], g_q[1]) * HEAD_DIM**-0.5
        g_k = g_k * HEAD_DIM**-0.5
        gq_s[:, cut] = turn(g_q, cos_sel[...], -sin_sel[...]).astype(LOW)
        gk_s[:, cut] = turn(g_k, cos[...], -sin[...]).astype(LOW)
        gv_s[:, cut] = g_v.astype(LOW)
    rows = tok[...]
    spread(dq_o, dot_tn(tok_sel[...], gq_s[...]), 1)
    spread(dk_o, dot_tn(rows, gk_s[...]), 2)
    spread(dv_o, dot_tn(rows, gv_s[...]), 3)
    small_o[1:2, 0:local] = col_sum(gq_s[...].astype(F32))
    small_o[1:2, local : 2 * local] = col_sum(gk_s[...].astype(F32))
    small_o[1:2, 2 * local : 3 * local] = col_sum(gv_s[...].astype(F32))
    gq_full = dot_tn(hot, gq_s[...]).astype(LOW)
    part_o[...] = dot_nt(gq_full, w_qkv[0]) + dot_nt(gk_s[...], w_qkv[1]) + dot_nt(gv_s[...], w_qkv[2])


def join_kernel(mine, other, pos, g_pre, out_o):
    hot = one_hot(pos, mine.shape[0]).astype(F32)
    spread = lax.dot_general(
        hot, g_pre[...], (((0,), (0,)), ((), ())), precision=lax.Precision.HIGHEST, preferred_element_type=F32
    )
    out_o[...] = mine[...] + other[...] + spread


def attend_kernel(query, keys, values, w_out, attn_o, ctx_s):
    pairs = query.shape[1] // PAIR
    for j in range(pairs):
        cut = slice(j * PAIR, (j + 1) * PAIR)
        q_pair = query[:, cut].astype(F32)
        lead = first_head(q_pair.shape)
        parts = []
        for side in range(2):
            chosen = jnp.where(lead if side == 0 else ~lead, q_pair, 0.0).astype(LOW)
            prob = softmax_of(dot_nt(chosen, keys[:, cut]) * HEAD_DIM**-0.5)
            parts.append(dot(prob.astype(LOW), values[:, cut]))
        ctx_s[:, cut] = jnp.where(lead, parts[0], parts[1]).astype(LOW)
    attn_o[...] = dot(ctx_s[...], w_out[...])


def feed_kernel(mine, other, tok, b_out, gain, shift, w_in, b_in, w_back, one_o, part_o):
    h_pre = tok[...].astype(F32) + (mine[...] + other[...] + b_out[...])
    hat, _ = center_of(h_pre)
    h_one = hat * gain[0:1, :] + shift[0:1, :]
    one_o[...] = h_one
    hidden = dot(h_one.astype(LOW), w_in[...]) + b_in[...]
    part_o[...] = dot((hidden * cdf_of(hidden)).astype(LOW), w_back[...])


def last_kernel(mine, other, h_one, b_back, gain, shift, out_o):
    z_sum = h_one[...] + (mine[...] + other[...] + b_back[...])
    hat, _ = center_of(z_sum)
    out_o[...] = (hat * gain[1:2, :] + shift[1:2, :]).astype(LOW)


def grads_kernel(h_a, h_b, g_a, g_b, w_in, b_in, w_back, sel_in, sel_back, din_o, dback_o):
    blocks, chunk = din_o.shape[:2]
    h_low = jnp.concatenate([h_a[...], h_b[...]], 0).astype(LOW)
    g_low = jnp.concatenate([g_a[...], g_b[...]], 0).astype(LOW)
    hidden = dot(h_low, w_in[...]) + b_in[...]
    cdf = cdf_of(hidden)
    act = (hidden * cdf).astype(LOW)
    grad_u = (dot_nt(g_low, w_back[...]) * gelu_slope(hidden, cdf)).astype(LOW)
    h_cols = dot(h_low, sel_in[...]).astype(LOW)
    g_cols = dot(g_low, sel_back[...]).astype(LOW)
    d_in = dot_tn(h_cols, grad_u)
    d_back = dot_tn(g_cols, act)
    for c in range(blocks):
        din_o[c] = d_in[c * chunk : (c + 1) * chunk]
        dback_o[c] = d_back[c * chunk : (c + 1) * chunk]


def call(kernel, outs, *args, scalars=0, scratch=()):
    specs = [pl.BlockSpec(memory_space=pltpu.SMEM)] * scalars
    specs += [pl.BlockSpec(memory_space=pltpu.VMEM)] * (len(args) - scalars)
    shapes = [jax.ShapeDtypeStruct(*item) for item in outs]
    result = pl.pallas_call(
        kernel,
        out_shape=shapes if len(shapes) > 1 else shapes[0],
        in_specs=specs,
        scratch_shapes=list(scratch),
        name=kernel.__name__,
    )(*args)
    return result


def shards(
    count,
    tokens,
    cotangent,
    masked_pos,
    w_qkv,
    b_qkv,
    w_out,
    b_out,
    w_in,
    b_in,
    w_back,
    b_back,
    ln_gain,
    ln_bias,
):
    _, length, width = tokens.shape
    local = w_qkv.shape[2]
    hidden = w_in.shape[1]
    slots = masked_pos.shape[1]
    heads = local // HEAD_DIM
    bits = count.bit_length() - 1
    chunk = width // count
    near = count // 4
    near_bits = bits - 2
    me = lax.axis_index("dp")
    core = lax.axis_index("mp").astype(jnp.int32)[None]
    cos, sin = tables(length)

    def flip(value):
        return lax.ppermute(value, "mp", [(0, 1), (1, 0)])

    def across(value, bit):
        return lax.ppermute(value, "dp", [(i, i ^ (1 << bit)) for i in range(count)])

    def halve(value, order):
        for bit in order:
            keep = value.shape[0] // 2
            value = value[:keep] + across(value[keep:], bit)
        return value[0]

    def slot_of(index, order):
        total = jnp.zeros_like(index)
        for at, bit in enumerate(order):
            total = total + (((index >> bit) & 1) << (len(order) - 1 - at))
        return total

    z_low, z_high = bits - 2, bits - 1
    rest = list(range(2, near_bits))
    order_out = [0, z_low, 1] + rest + [z_high]
    order_q = [0, 1] + rest + [z_low, z_high]
    order_k = [1, 0] + rest + [z_low, z_high]
    order_v = [z_low, 1, 0] + rest + [z_high]
    order_in = [0, 1] + rest
    order_back = [1, 0] + rest
    delta = jnp.arange(count, dtype=jnp.int32) ^ me.astype(jnp.int32)
    place = jnp.stack([slot_of(delta, o) for o in (order_out, order_q, order_k, order_v)])

    def columns(order):
        index = jnp.arange(width, dtype=jnp.int32)
        number = index // chunk
        spot = slot_of((number % near) ^ (me % near).astype(jnp.int32), order) * chunk + index % chunk
        spot = jnp.where(number // near == me // near, spot, -1)
        return (spot[:, None] == jnp.arange(near * chunk, dtype=jnp.int32)).astype(LOW)

    sel_in = columns(order_in)
    sel_back = columns(order_back)

    def gather_far(value):
        others = [
            lax.ppermute(value, "dp", [(i, (i + step * near) % count) for i in range(count)]) for step in (1, 3, 2)
        ]
        return jnp.concatenate([value] + others, 0)

    tok = tokens[0]
    cot = cotangent[0]
    pos = masked_pos.reshape(slots, 1)
    b_out, b_in, b_back = b_out[None], b_in[None], b_back[None]

    query, keys, values, q_sel, tok_sel, cos_sel, sin_sel, prob, ctx_sel, attn = call(
        front_kernel,
        [
            ((length, local), LOW),
            ((length, local), LOW),
            ((length, local), LOW),
            ((slots, local), LOW),
            ((slots, width), LOW),
            ((slots, PAIR), F32),
            ((slots, PAIR), F32),
            ((heads, slots, length), F32),
            ((slots, local), LOW),
            ((slots, width), F32),
        ],
        tok, w_qkv, b_qkv, cos, sin, pos, w_out,
    )
    h_one, part, hat, scale, slope, h_half = call(
        mid_kernel,
        [
            ((slots, width), F32),
            ((slots, width), F32),
            ((slots, width), F32),
            ((slots, 1), F32),
            ((slots, hidden), F32),
            ((slots // 2, width), F32),
        ],
        core, attn, flip(attn), tok_sel, b_out, ln_gain, ln_bias, w_in, b_in, w_back,
        scalars=1,
    )
    h_mine = gather_far(h_half)
    h_other = flip(h_mine)
    grad_z, g_half, part, small = call(
        turn_kernel,
        [
            ((slots, width), F32),
            ((slots // 2, width), F32),
            ((slots, width), F32),
            ((8, hidden), F32),
        ],
        core, part, flip(part), h_one, b_back, ln_gain, cot, pos, slope, w_in, w_back,
        scalars=1,
    )
    grad_h_other = flip(part)
    g_mine = gather_far(g_half)
    g_other = flip(g_mine)
    shape = ((count, chunk, local), F32)
    dw_q, dw_k, dw_v, dw_out, back_part, small, g_pre = call(
        back_kernel,
        [shape, shape, shape, shape, ((length, width), F32), ((8, hidden), F32), ((slots, width), F32)],
        place, part, grad_h_other, grad_z, hat, scale, ln_gain, tok, tok_sel, ctx_sel, w_out, q_sel, keys, values,
        prob, w_qkv, pos, cos, sin, cos_sel, sin_sel, small,
        scalars=1,
        scratch=[
            pltpu.VMEM((length, local), LOW),
            pltpu.VMEM((length, local), LOW),
            pltpu.VMEM((slots, local), LOW),
        ],
    )
    shape = ((near, chunk, hidden), F32)
    dw_in, dw_back = call(
        grads_kernel, [shape, shape], h_mine, h_other, g_mine, g_other, w_in, b_in, w_back, sel_in, sel_back
    )
    query, g_pre = lax.optimization_barrier((query, g_pre))
    attn = call(
        attend_kernel, [((length, width), F32)], query, keys, values, w_out,
        scratch=[pltpu.VMEM((length, local), LOW)],
    )
    h_full, part = call(
        feed_kernel,
        [((length, width), F32), ((length, width), F32)],
        attn, flip(attn), tok, b_out, ln_gain, ln_bias, w_in, b_in, w_back,
    )
    output = call(
        last_kernel, [((length, width), LOW)], part, flip(part), h_full, b_back, ln_gain, ln_bias
    )
    grad_tokens = call(join_kernel, [((length, width), F32)], back_part, flip(back_part), pos, g_pre)
    for bit in range(bits):
        small = small + across(small, bit)
    sum_out = halve(dw_out, order_out).T
    sum_qkv = jnp.stack([halve(dw_q, order_q), halve(dw_k, order_k), halve(dw_v, order_v)])
    sum_in = halve(dw_in, order_in)
    sum_back = halve(dw_back, order_back).T
    return (
        output[None],
        grad_tokens[None],
        sum_qkv,
        small[1, : 3 * local].reshape(3, local),
        sum_out,
        small[2, :width],
        sum_in,
        small[0],
        sum_back,
        small[2, width:],
        small[3].reshape(2, width),
        small[4].reshape(2, width),
    )


def solution(mesh):
    in_specs = (
        P("dp", None, None),
        P("dp", None, None),
        P("dp", None),
        P(None, None, "mp"),
        P(None, "mp"),
        P("mp", None),
        P(),
        P(None, "mp"),
        P("mp"),
        P("mp", None),
        P(),
        P(),
        P(),
    )
    out_specs = (
        P("dp", None, None),
        P("dp", None, None),
        P(None, "dp", "mp"),
        P(None, "mp"),
        P("mp", "dp"),
        P(),
        P("dp", "mp"),
        P("mp"),
        P("mp", "dp"),
        P(),
        P(),
        P(),
    )
    count = mesh.shape["dp"]

    def body(*args):
        return shards(count, *args)

    return jax.shard_map(body, mesh=mesh, in_specs=in_specs, out_specs=out_specs, check_vma=False)
```

```python
import jax
import jax.numpy as jnp
import numpy as np
from jax import lax
from jax.experimental import pallas as pl
from jax.experimental.pallas import tpu as pltpu
from jax.sharding import PartitionSpec as P


HEAD_DIM = 64
PAIR = 2 * HEAD_DIM
EPS = 1e-06
F32 = jnp.float32
LOW = jnp.bfloat16


def tables(length):
    half = HEAD_DIM // 2
    freq = np.float32(10000.0) ** (-np.arange(half).astype(np.float32) / np.float32(half))
    angle = np.arange(length).astype(np.float32)[:, None] * freq.astype(np.float32)
    cosine = np.cos(angle).astype(np.float32)
    sine = np.sin(angle).astype(np.float32)
    cos_pair = np.concatenate([cosine] * 4, 1)
    sin_pair = np.concatenate([-sine, sine, -sine, sine], 1)
    return jnp.asarray(cos_pair), jnp.asarray(sin_pair)


def dot(left, right):
    return jnp.dot(left, right, preferred_element_type=F32)


def dot_nt(left, right):
    return lax.dot_general(left, right, (((1,), (1,)), ((), ())), preferred_element_type=F32)


def dot_tn(left, right):
    return lax.dot_general(left, right, (((0,), (0,)), ((), ())), preferred_element_type=F32)


def first_half(shape):
    return lax.broadcasted_iota(jnp.int32, shape, 1) % HEAD_DIM < HEAD_DIM // 2


def first_head(shape):
    return lax.broadcasted_iota(jnp.int32, shape, 1) < HEAD_DIM


def swapped(value):
    half = HEAD_DIM // 2
    ahead = pltpu.roll(value, PAIR - half, 1)
    behind = pltpu.roll(value, half, 1)
    return jnp.where(first_half(value.shape), ahead, behind)


def turn(value, cosine, sine):
    return value * cosine + swapped(value) * sine


def center_of(value):
    center = value - jnp.mean(value, -1, keepdims=True)
    scale = lax.rsqrt(jnp.mean(center * center, -1, keepdims=True) + EPS)
    return center * scale, scale


def norm_back(grad, hat, scale, gain):
    grad_hat = grad * gain
    mean_one = jnp.mean(grad_hat, -1, keepdims=True)
    mean_two = jnp.mean(grad_hat * hat, -1, keepdims=True)
    return scale * (grad_hat - mean_one - hat * mean_two)


def cdf_of(value):
    return 0.5 * (1.0 + lax.erf(value * np.float32(0.5**0.5)))


def gelu_slope(value, cdf):
    return cdf + value * (np.float32(1 / (2 * np.pi) ** 0.5) * jnp.exp(-0.5 * value * value))


def one_hot(pos_ref, length):
    pos = pos_ref[...]
    return lax.broadcasted_iota(jnp.int32, (pos.shape[0], length), 1) == pos


def col_sum(value):
    return jnp.sum(value, 0, keepdims=True)


def softmax_of(scores):
    expo = jnp.exp(scores - jnp.max(scores, -1, keepdims=True))
    return expo / jnp.sum(expo, -1, keepdims=True)


def front_kernel(
    tok, w_qkv, b_qkv, cos, sin, pos, w_out, q_o, k_o, v_o, qs_o, ts_o, cs_o, ss_o, prob_o, ctx_o, attn_o
):
    length = tok.shape[0]
    local = w_qkv.shape[2]
    pairs = local // PAIR
    hot_f = one_hot(pos, length).astype(F32)
    hot = hot_f.astype(LOW)
    rows = tok[...]
    ts_o[...] = dot(hot, rows).astype(LOW)
    cs_o[...] = jnp.dot(hot_f, cos[...], precision=lax.Precision.HIGHEST)
    ss_o[...] = jnp.dot(hot_f, sin[...], precision=lax.Precision.HIGHEST)
    pre_q = dot(rows, w_qkv[0]) + b_qkv[0:1, :]
    pre_k = dot(rows, w_qkv[1]) + b_qkv[1:2, :]
    v_o[...] = (dot(rows, w_qkv[2]) + b_qkv[2:3, :]).astype(LOW)
    for j in range(pairs):
        cut = slice(j * PAIR, (j + 1) * PAIR)
        q_o[:, cut] = turn(pre_q[:, cut], cos[...], sin[...]).astype(LOW)
        k_o[:, cut] = turn(pre_k[:, cut], cos[...], sin[...]).astype(LOW)
    qs_o[...] = dot(hot, q_o[...]).astype(LOW)
    for j in range(pairs):
        cut = slice(j * PAIR, (j + 1) * PAIR)
        query = qs_o[:, cut]
        keys = k_o[:, cut]
        values = v_o[:, cut]
        lead = first_head(query.shape)
        parts = []
        for side in range(2):
            chosen = jnp.where(lead if side == 0 else ~lead, query.astype(F32), 0.0).astype(LOW)
            prob = softmax_of(dot_nt(chosen, keys) * HEAD_DIM**-0.5)
            prob_o[2 * j + side] = prob
            parts.append(dot(prob.astype(LOW), values))
        ctx_o[:, cut] = jnp.where(lead, parts[0], parts[1]).astype(LOW)
    attn_o[...] = dot(ctx_o[...], w_out[...])


def mid_kernel(
    mine, other, tok, b_out, gain, shift, w_in, b_in, w_back, one_o, part_o, hat_o, scale_o, slope_o
):
    h_pre = tok[...].astype(F32) + (mine[...] + other[...] + b_out[...])
    hat, scale = center_of(h_pre)
    h_one = hat * gain[0:1, :] + shift[0:1, :]
    one_o[...] = h_one
    hidden = dot(h_one.astype(LOW), w_in[...]) + b_in[...]
    cdf = cdf_of(hidden)
    part_o[...] = dot((hidden * cdf).astype(LOW), w_back[...])
    hat_o[...] = hat
    scale_o[...] = scale
    slope_o[...] = gelu_slope(hidden, cdf)


def turn_kernel(
    mpi, mine, other, h_one, b_back, gain, cot, pos, slope, w_in, w_back, gz_o, half_o, part_o, small_o
):
    width = h_one.shape[1]
    z_sum = h_one[...] + (mine[...] + other[...] + b_back[...])
    hat, scale = center_of(z_sum)
    grad = jnp.where(pos[...] >= 0, cot[...], 0.0)
    grad_z = norm_back(grad, hat, scale, gain[1:2, :])
    gz_o[...] = grad_z
    count = half_o.shape[0] // 2
    half_o[:count] = jnp.where(mpi[0] == 0, h_one[:count], h_one[count:])
    half_o[count:] = jnp.where(mpi[0] == 0, grad_z[:count], grad_z[count:])
    grad_y = grad_z.astype(LOW)
    grad_u = (dot_nt(grad_y, w_back[...]) * slope[...]).astype(LOW)
    part_o[...] = dot_nt(grad_u, w_in[...])
    small_o[...] = jnp.zeros(small_o.shape, F32)
    small_o[0:1, :] = col_sum(grad_u.astype(F32))
    small_o[2:3, width:] = col_sum(grad_y.astype(F32))
    small_o[3:4, width:] = col_sum(grad * hat)
    small_o[4:5, width:] = col_sum(grad)


def back_kernel(
    place, mine, other, grad_z, hat, scale, gain, tok, tok_sel, ctx, w_out, q_sel, keys, values, prob,
    cos, sin, cos_sel, sin_sel, small,
    a_keep, a_send, b_keep, b_send, gq_s, gk_s, gv_s, small_o, pre_o,
):
    _, width = tok.shape
    local = w_out.shape[0]
    pairs = local // PAIR
    near = a_keep.shape[0]
    blocks = 2 * near
    chunk = width // blocks
    grad_h = mine[...] + other[...] + grad_z[...]
    g_pre = norm_back(grad_h, hat[...], scale[...], gain[0:1, :])
    pre_o[...] = g_pre
    g_attn = g_pre.astype(LOW)
    small_o[...] = small[...]
    small_o[2:3, :width] = col_sum(g_attn.astype(F32))
    small_o[3:4, :width] = col_sum(grad_h * hat[...])
    small_o[4:5, :width] = col_sum(grad_h)

    def spread(keep, send, order, left, right):
        for c in range(blocks):
            rows_of = slice(c * chunk, (c + 1) * chunk)
            spot = place[order, c]

            @pl.when(spot < near)
            def _():
                keep[spot, :, :local] = left[rows_of]
                keep[spot, :, local:] = right[rows_of]

            @pl.when(spot >= near)
            def _():
                send[spot - near, :, :local] = left[rows_of]
                send[spot - near, :, local:] = right[rows_of]

    dw_out = dot_tn(g_attn, ctx[...])
    g_ctx = dot_nt(g_attn, w_out[...]).astype(LOW)
    for j in range(pairs):
        cut = slice(j * PAIR, (j + 1) * PAIR)
        key_pair = keys[:, cut]
        value_pair = values[:, cut]
        query_pair = q_sel[:, cut].astype(F32)
        ctx_pair = g_ctx[:, cut].astype(F32)
        lead = first_head(query_pair.shape)
        g_q, g_k, g_v = [], None, None
        for side in range(2):
            keep = lead if side == 0 else ~lead
            q_one = jnp.where(keep, query_pair, 0.0).astype(LOW)
            c_one = jnp.where(keep, ctx_pair, 0.0).astype(LOW)
            weight = prob[2 * j + side]
            g_prob = dot_nt(c_one, value_pair)
            inner = jnp.sum(weight * g_prob, -1, keepdims=True)
            g_score = (weight * (g_prob - inner)).astype(LOW)
            add_v = dot_tn(weight.astype(LOW), c_one)
            add_k = dot_tn(g_score, q_one)
            g_v = add_v if g_v is None else g_v + add_v
            g_k = add_k if g_k is None else g_k + add_k
            g_q.append(dot(g_score, key_pair))
        g_q = jnp.where(lead, g_q[0], g_q[1]) * HEAD_DIM**-0.5
        g_k = g_k * HEAD_DIM**-0.5
        gq_s[:, cut] = turn(g_q, cos_sel[...], -sin_sel[...]).astype(LOW)
        gk_s[:, cut] = turn(g_k, cos[...], -sin[...]).astype(LOW)
        gv_s[:, cut] = g_v.astype(LOW)
    rows = tok[...]
    spread(a_keep, a_send, 0, dw_out, dot_tn(tok_sel[...], gq_s[...]))
    spread(b_keep, b_send, 1, dot_tn(rows, gk_s[...]), dot_tn(rows, gv_s[...]))
    small_o[1:2, 0:local] = col_sum(gq_s[...].astype(F32))
    small_o[1:2, local : 2 * local] = col_sum(gk_s[...].astype(F32))
    small_o[1:2, 2 * local : 3 * local] = col_sum(gv_s[...].astype(F32))


def tokens_kernel(mpi, g_q, g_k, g_v, w_qkv, pos, g_pre, part_o):
    hot = one_hot(pos, g_k.shape[0]).astype(F32).astype(LOW)
    gq_full = dot_tn(hot, g_q[...]).astype(LOW)
    total = dot_nt(gq_full, w_qkv[0]) + dot_nt(g_k[...], w_qkv[1]) + dot_nt(g_v[...], w_qkv[2])
    part_o[...] = total

    @pl.when(mpi[0] == 0)
    def _():
        left = g_pre[...]
        spread = part_o[...]
        for _ in range(3):
            piece = left.astype(LOW)
            left = left - piece.astype(F32)
            spread = spread + dot_tn(hot, piece)
        part_o[...] = spread


def attend_kernel(query, keys, values, w_out, attn_o, ctx_s):
    pairs = query.shape[1] // PAIR
    for j in range(pairs):
        cut = slice(j * PAIR, (j + 1) * PAIR)
        q_pair = query[:, cut].astype(F32)
        lead = first_head(q_pair.shape)
        parts = []
        for side in range(2):
            chosen = jnp.where(lead if side == 0 else ~lead, q_pair, 0.0).astype(LOW)
            prob = softmax_of(dot_nt(chosen, keys[:, cut]) * HEAD_DIM**-0.5)
            parts.append(dot(prob.astype(LOW), values[:, cut]))
        ctx_s[:, cut] = jnp.where(lead, parts[0], parts[1]).astype(LOW)
    attn_o[...] = dot(ctx_s[...], w_out[...])


def feed_kernel(mine, other, tok, b_out, gain, shift, w_in, b_in, w_back, one_o, part_o):
    h_pre = tok[...].astype(F32) + (mine[...] + other[...] + b_out[...])
    hat, _ = center_of(h_pre)
    h_one = hat * gain[0:1, :] + shift[0:1, :]
    one_o[...] = h_one
    hidden = dot(h_one.astype(LOW), w_in[...]) + b_in[...]
    part_o[...] = dot((hidden * cdf_of(hidden)).astype(LOW), w_back[...])


def last_kernel(mine, other, h_one, b_back, gain, shift, out_o):
    z_sum = h_one[...] + (mine[...] + other[...] + b_back[...])
    hat, _ = center_of(z_sum)
    out_o[...] = (hat * gain[1:2, :] + shift[1:2, :]).astype(LOW)


def grads_kernel(
    h_one, grad_z, far_a, far_b, far_c, flipped, w_in, b_in, w_back, sel_in, sel_back,
    in_keep, in_send, back_keep, back_send,
):
    near, chunk = in_keep.shape[:2]
    part = far_a.shape[0] // 2
    fars = [far_a[...], far_b[...], far_c[...], flipped[...]]
    h_rows = [h_one[...]]
    g_rows = [grad_z[...]]
    for block in fars:
        for start in range(0, block.shape[0], 2 * part):
            h_rows.append(block[start : start + part])
            g_rows.append(block[start + part : start + 2 * part])
    h_low = jnp.concatenate(h_rows, 0).astype(LOW)
    g_low = jnp.concatenate(g_rows, 0).astype(LOW)
    hidden = dot(h_low, w_in[...]) + b_in[...]
    cdf = cdf_of(hidden)
    act = (hidden * cdf).astype(LOW)
    grad_u = (dot_nt(g_low, w_back[...]) * gelu_slope(hidden, cdf)).astype(LOW)
    h_cols = dot(h_low, sel_in[...]).astype(LOW)
    g_cols = dot(g_low, sel_back[...]).astype(LOW)
    d_in = dot_tn(h_cols, grad_u)
    d_back = dot_tn(g_cols, act)
    for c in range(near):
        in_keep[c] = d_in[c * chunk : (c + 1) * chunk]
        back_keep[c] = d_back[c * chunk : (c + 1) * chunk]
        in_send[c] = d_in[(near + c) * chunk : (near + c + 1) * chunk]
        back_send[c] = d_back[(near + c) * chunk : (near + c + 1) * chunk]


def finish_feed_kernel(keep_in, got_in, keep_back, got_back, in_o, back_o):
    in_o[...] = keep_in[0] + got_in[0]
    back_o[...] = keep_back[0] + got_back[0]


def finish_heads_kernel(keep_a, got_a, keep_b, got_b, out_o, qkv_o):
    local = out_o.shape[1]
    out_o[...] = keep_a[0, :, :local] + got_a[0, :, :local]
    qkv_o[0] = keep_a[0, :, local:] + got_a[0, :, local:]
    qkv_o[1] = keep_b[0, :, :local] + got_b[0, :, :local]
    qkv_o[2] = keep_b[0, :, local:] + got_b[0, :, local:]


def call(kernel, outs, *args, scalars=0, scratch=()):
    specs = [pl.BlockSpec(memory_space=pltpu.SMEM)] * scalars
    specs += [pl.BlockSpec(memory_space=pltpu.VMEM)] * (len(args) - scalars)
    shapes = [jax.ShapeDtypeStruct(*item) for item in outs]
    result = pl.pallas_call(
        kernel,
        out_shape=shapes if len(shapes) > 1 else shapes[0],
        in_specs=specs,
        scratch_shapes=list(scratch),
    )
    return result(*args)


def shards(
    count,
    tokens,
    cotangent,
    masked_pos,
    w_qkv,
    b_qkv,
    w_out,
    b_out,
    w_in,
    b_in,
    w_back,
    b_back,
    ln_gain,
    ln_bias,
):
    _, length, width = tokens.shape
    local = w_qkv.shape[2]
    hidden = w_in.shape[1]
    slots = masked_pos.shape[1]
    heads = local // HEAD_DIM
    bits = count.bit_length() - 1
    chunk = width // count
    near = count // 4
    near_bits = bits - 2
    me = lax.axis_index("dp")
    core = lax.axis_index("mp").astype(jnp.int32)[None]
    cos, sin = tables(length)

    def flip(value):
        return lax.ppermute(value, "mp", [(0, 1), (1, 0)])

    def across(value, bit):
        return lax.ppermute(value, "dp", [(i, i ^ (1 << bit)) for i in range(count)])

    def halve(keep, send, order):
        for bit in order:
            got = across(send, bit)
            half = got.shape[0] // 2
            if half:
                send = keep[half:] + got[half:]
                keep = keep[:half] + got[:half]
        return keep, got

    def slot_of(index, order):
        total = jnp.zeros_like(index)
        for at, bit in enumerate(order):
            total = total + (((index >> bit) & 1) << (len(order) - 1 - at))
        return total

    z_low, z_high = bits - 2, bits - 1
    rest = list(range(2, near_bits))
    order_a = [0, 1] + rest + [z_low, z_high]
    order_b = [1, z_low, 0] + rest + [z_high]
    order_in = [0, 1] + rest
    order_back = [1, 0] + rest
    delta = jnp.arange(count, dtype=jnp.int32) ^ me.astype(jnp.int32)
    place = jnp.stack([slot_of(delta, o) for o in (order_a, order_b)])

    def columns(order):
        index = jnp.arange(width, dtype=jnp.int32)
        number = index // chunk
        spot = slot_of((number % near) ^ (me % near).astype(jnp.int32), order) * chunk + index % chunk
        spot = jnp.where(number // near == me // near, spot, -1)
        return (spot[:, None] == jnp.arange(near * chunk, dtype=jnp.int32)).astype(LOW)

    sel_in = columns(order_in)
    sel_back = columns(order_back)

    def gather_far(value):
        return [
            lax.ppermute(value, "dp", [(i, (i + step * near) % count) for i in range(count)])
            for step in (2, 1, 3)
        ]

    tok = tokens[0]
    cot = cotangent[0]
    pos = masked_pos.reshape(slots, 1)
    b_out, b_in, b_back = b_out[None], b_in[None], b_back[None]

    query, keys, values, q_sel, tok_sel, cos_sel, sin_sel, prob, ctx_sel, attn = call(
        front_kernel,
        [
            ((length, local), LOW),
            ((length, local), LOW),
            ((length, local), LOW),
            ((slots, local), LOW),
            ((slots, width), LOW),
            ((slots, PAIR), F32),
            ((slots, PAIR), F32),
            ((heads, slots, length), F32),
            ((slots, local), LOW),
            ((slots, width), F32),
        ],
        tok, w_qkv, b_qkv, cos, sin, pos, w_out,
    )
    h_one, part, hat, scale, slope = call(
        mid_kernel,
        [
            ((slots, width), F32),
            ((slots, width), F32),
            ((slots, width), F32),
            ((slots, 1), F32),
            ((slots, hidden), F32),
        ],
        attn, flip(attn), tok_sel, b_out, ln_gain, ln_bias, w_in, b_in, w_back,
    )
    grad_z, half_rows, part, small = call(
        turn_kernel,
        [
            ((slots, width), F32),
            ((slots, width), F32),
            ((slots, width), F32),
            ((8, hidden), F32),
        ],
        core, part, flip(part), h_one, b_back, ln_gain, cot, pos, slope, w_in, w_back,
        scalars=1,
    )
    grad_h_other = flip(part)
    far = gather_far(half_rows)
    far_flipped = flip(jnp.concatenate(far, 0))
    shape = ((count // 2, chunk, 2 * local), F32)
    a_keep, a_send, b_keep, b_send, g_q, g_k, g_v, small, g_pre = call(
        back_kernel,
        [
            shape,
            shape,
            shape,
            shape,
            ((slots, local), LOW),
            ((length, local), LOW),
            ((length, local), LOW),
            ((8, hidden), F32),
            ((slots, width), F32),
        ],
        place, part, grad_h_other, grad_z, hat, scale, ln_gain, tok, tok_sel, ctx_sel, w_out, q_sel, keys, values,
        prob, cos, sin, cos_sel, sin_sel, small,
        scalars=1,
    )
    back_part = call(tokens_kernel, [((length, width), F32)], core, g_q, g_k, g_v, w_qkv, pos, g_pre, scalars=1)
    shape = ((near // 2, chunk, hidden), F32)
    in_keep, in_send, back_keep, back_send = call(
        grads_kernel, [shape] * 4, h_one, grad_z, *far, far_flipped, w_in, b_in, w_back, sel_in, sel_back
    )
    query, g_pre = lax.optimization_barrier((query, g_pre))
    attn = call(
        attend_kernel, [((length, width), F32)], query, keys, values, w_out,
        scratch=[pltpu.VMEM((length, local), LOW)],
    )
    h_full, part = call(
        feed_kernel,
        [((length, width), F32), ((length, width), F32)],
        attn, flip(attn), tok, b_out, ln_gain, ln_bias, w_in, b_in, w_back,
    )
    output = call(
        last_kernel, [((length, width), LOW)], part, flip(part), h_full, b_back, ln_gain, ln_bias
    )
    grad_tokens = jnp.add(back_part, flip(back_part))
    for bit in range(bits):
        small = small + across(small, bit)
    last_a = halve(a_keep, a_send, order_a)
    last_b = halve(b_keep, b_send, order_b)
    last_in = halve(in_keep, in_send, order_in)
    last_back = halve(back_keep, back_send, order_back)
    sum_in, sum_back = call(
        finish_feed_kernel, [((chunk, hidden), F32)] * 2, *last_in, *last_back
    )
    sum_out, sum_qkv = call(
        finish_heads_kernel, [((chunk, local), F32), ((3, chunk, local), F32)], *last_a, *last_b
    )
    return (
        output[None],
        grad_tokens[None],
        sum_qkv,
        small[1, : 3 * local].reshape(3, local),
        sum_out.T,
        small[2, :width],
        sum_in,
        small[0],
        sum_back.T,
        small[2, width:],
        small[3].reshape(2, width),
        small[4].reshape(2, width),
    )


def solution(mesh):
    in_specs = (
        P("dp", None, None),
        P("dp", None, None),
        P("dp", None),
        P(None, None, "mp"),
        P(None, "mp"),
        P("mp", None),
        P(),
        P(None, "mp"),
        P("mp"),
        P("mp", None),
        P(),
        P(),
        P(),
    )
    out_specs = (
        P("dp", None, None),
        P("dp", None, None),
        P(None, "dp", "mp"),
        P(None, "mp"),
        P("mp", "dp"),
        P(),
        P("dp", "mp"),
        P("mp"),
        P("mp", "dp"),
        P(),
        P(),
        P(),
    )
    count = mesh.shape["dp"]

    def body(*args):
        return shards(count, *args)

    return jax.shard_map(body, mesh=mesh, in_specs=in_specs, out_specs=out_specs, check_vma=False)
```

```python
import jax
import jax.numpy as jnp
import numpy as np
from jax import lax
from jax.experimental import pallas as pl
from jax.experimental.pallas import tpu as pltpu
from jax.sharding import PartitionSpec as P


HEAD_DIM = 64
PAIR = 2 * HEAD_DIM
EPS = 1e-06
F32 = jnp.float32
LOW = jnp.bfloat16


def tables(length):
    half = HEAD_DIM // 2
    freq = np.float32(10000.0) ** (-np.arange(half).astype(np.float32) / np.float32(half))
    angle = np.arange(length).astype(np.float32)[:, None] * freq.astype(np.float32)
    cosine = np.cos(angle).astype(np.float32)
    sine = np.sin(angle).astype(np.float32)
    cos_pair = np.concatenate([cosine] * 4, 1)
    sin_pair = np.concatenate([-sine, sine, -sine, sine], 1)
    return jnp.asarray(cos_pair), jnp.asarray(sin_pair)


def dot(left, right):
    return jnp.dot(left, right, preferred_element_type=F32)


def dot_nt(left, right):
    return lax.dot_general(left, right, (((1,), (1,)), ((), ())), preferred_element_type=F32)


def dot_tn(left, right):
    return lax.dot_general(left, right, (((0,), (0,)), ((), ())), preferred_element_type=F32)


def first_half(shape):
    return lax.broadcasted_iota(jnp.int32, shape, 1) % HEAD_DIM < HEAD_DIM // 2


def first_head(shape):
    return lax.broadcasted_iota(jnp.int32, shape, 1) < HEAD_DIM


def swapped(value):
    half = HEAD_DIM // 2
    ahead = pltpu.roll(value, PAIR - half, 1)
    behind = pltpu.roll(value, half, 1)
    return jnp.where(first_half(value.shape), ahead, behind)


def turn(value, cosine, sine):
    return value * cosine + swapped(value) * sine


def center_of(value):
    center = value - jnp.mean(value, -1, keepdims=True)
    scale = lax.rsqrt(jnp.mean(center * center, -1, keepdims=True) + EPS)
    return center * scale, scale


def norm_back(grad, hat, scale, gain):
    grad_hat = grad * gain
    mean_one = jnp.mean(grad_hat, -1, keepdims=True)
    mean_two = jnp.mean(grad_hat * hat, -1, keepdims=True)
    return scale * (grad_hat - mean_one - hat * mean_two)


def cdf_of(value):
    return 0.5 * (1.0 + lax.erf(value * np.float32(0.5**0.5)))


def gelu_slope(value, cdf):
    return cdf + value * (np.float32(1 / (2 * np.pi) ** 0.5) * jnp.exp(-0.5 * value * value))


def one_hot(pos_ref, length):
    pos = pos_ref[...]
    return lax.broadcasted_iota(jnp.int32, (pos.shape[0], length), 1) == pos


def col_sum(value):
    return jnp.sum(value, 0, keepdims=True)


def softmax_of(scores):
    expo = jnp.exp(scores - jnp.max(scores, -1, keepdims=True))
    return expo / jnp.sum(expo, -1, keepdims=True)


def front_kernel(
    tok, w_qkv, b_qkv, cos, sin, pos, w_out, q_o, k_o, v_o, qs_o, ts_o, cs_o, ss_o, prob_o, ctx_o, attn_o
):
    length = tok.shape[0]
    local = w_qkv.shape[2]
    pairs = local // PAIR
    hot_f = one_hot(pos, length).astype(F32)
    hot = hot_f.astype(LOW)
    rows = tok[...]
    ts_o[...] = dot(hot, rows).astype(LOW)
    cs_o[...] = jnp.dot(hot_f, cos[...], precision=lax.Precision.HIGHEST)
    ss_o[...] = jnp.dot(hot_f, sin[...], precision=lax.Precision.HIGHEST)
    pre_q = dot(rows, w_qkv[0]) + b_qkv[0:1, :]
    pre_k = dot(rows, w_qkv[1]) + b_qkv[1:2, :]
    v_o[...] = (dot(rows, w_qkv[2]) + b_qkv[2:3, :]).astype(LOW)
    for j in range(pairs):
        cut = slice(j * PAIR, (j + 1) * PAIR)
        q_o[:, cut] = turn(pre_q[:, cut], cos[...], sin[...]).astype(LOW)
        k_o[:, cut] = turn(pre_k[:, cut], cos[...], sin[...]).astype(LOW)
    qs_o[...] = dot(hot, q_o[...]).astype(LOW)
    for j in range(pairs):
        cut = slice(j * PAIR, (j + 1) * PAIR)
        query = qs_o[:, cut]
        keys = k_o[:, cut]
        values = v_o[:, cut]
        lead = first_head(query.shape)
        parts = []
        for side in range(2):
            chosen = jnp.where(lead if side == 0 else ~lead, query.astype(F32), 0.0).astype(LOW)
            prob = softmax_of(dot_nt(chosen, keys) * HEAD_DIM**-0.5)
            prob_o[2 * j + side] = prob
            parts.append(dot(prob.astype(LOW), values))
        ctx_o[:, cut] = jnp.where(lead, parts[0], parts[1]).astype(LOW)
    attn_o[...] = dot(ctx_o[...], w_out[...])


def mid_kernel(
    mine, other, tok, b_out, gain, shift, w_in, b_in, w_back, one_o, part_o, hat_o, scale_o, slope_o
):
    h_pre = tok[...].astype(F32) + (mine[...] + other[...] + b_out[...])
    hat, scale = center_of(h_pre)
    h_one = hat * gain[0:1, :] + shift[0:1, :]
    one_o[...] = h_one
    hidden = dot(h_one.astype(LOW), w_in[...]) + b_in[...]
    cdf = cdf_of(hidden)
    part_o[...] = dot((hidden * cdf).astype(LOW), w_back[...])
    hat_o[...] = hat
    scale_o[...] = scale
    slope_o[...] = gelu_slope(hidden, cdf)


def turn_kernel(
    mpi, mine, other, h_one, b_back, gain, cot, pos, slope, w_in, w_back, gz_o, half_o, part_o, small_o
):
    width = h_one.shape[1]
    z_sum = h_one[...] + (mine[...] + other[...] + b_back[...])
    hat, scale = center_of(z_sum)
    grad = jnp.where(pos[...] >= 0, cot[...], 0.0)
    grad_z = norm_back(grad, hat, scale, gain[1:2, :])
    gz_o[...] = grad_z
    count = half_o.shape[0] // 2
    half_o[:count] = jnp.where(mpi[0] == 0, h_one[:count], h_one[count:])
    half_o[count:] = jnp.where(mpi[0] == 0, grad_z[:count], grad_z[count:])
    grad_y = grad_z.astype(LOW)
    grad_u = (dot_nt(grad_y, w_back[...]) * slope[...]).astype(LOW)
    part_o[...] = dot_nt(grad_u, w_in[...])
    small_o[...] = jnp.zeros(small_o.shape, F32)
    small_o[0:1, :] = col_sum(grad_u.astype(F32))
    small_o[2:3, width:] = col_sum(grad_y.astype(F32))
    small_o[3:4, width:] = col_sum(grad * hat)
    small_o[4:5, width:] = col_sum(grad)


def back_kernel(
    place, mine, other, grad_z, hat, scale, gain, tok, tok_sel, ctx, w_out, q_sel, keys, values, prob,
    cos, sin, cos_sel, sin_sel, small,
    a_keep, a_send, b_keep, b_send, gq_s, gk_s, gv_s, small_o, pre_o,
):
    _, width = tok.shape
    local = w_out.shape[0]
    pairs = local // PAIR
    near = a_keep.shape[0]
    blocks = 2 * near
    chunk = width // blocks
    grad_h = mine[...] + other[...] + grad_z[...]
    g_pre = norm_back(grad_h, hat[...], scale[...], gain[0:1, :])
    pre_o[...] = g_pre
    g_attn = g_pre.astype(LOW)
    small_o[...] = small[...]
    small_o[2:3, :width] = col_sum(g_attn.astype(F32))
    small_o[3:4, :width] = col_sum(grad_h * hat[...])
    small_o[4:5, :width] = col_sum(grad_h)

    def spread(keep, send, order, left, right):
        for c in range(blocks):
            rows_of = slice(c * chunk, (c + 1) * chunk)
            spot = place[order, c]

            @pl.when(spot < near)
            def _():
                keep[spot, :, :local] = left[rows_of]
                keep[spot, :, local:] = right[rows_of]

            @pl.when(spot >= near)
            def _():
                send[spot - near, :, :local] = left[rows_of]
                send[spot - near, :, local:] = right[rows_of]

    dw_out = dot_tn(g_attn, ctx[...])
    g_ctx = dot_nt(g_attn, w_out[...]).astype(LOW)
    for j in range(pairs):
        cut = slice(j * PAIR, (j + 1) * PAIR)
        key_pair = keys[:, cut]
        value_pair = values[:, cut]
        query_pair = q_sel[:, cut].astype(F32)
        ctx_pair = g_ctx[:, cut].astype(F32)
        lead = first_head(query_pair.shape)
        g_q, g_k, g_v = [], None, None
        for side in range(2):
            keep = lead if side == 0 else ~lead
            q_one = jnp.where(keep, query_pair, 0.0).astype(LOW)
            c_one = jnp.where(keep, ctx_pair, 0.0).astype(LOW)
            weight = prob[2 * j + side]
            g_prob = dot_nt(c_one, value_pair)
            inner = jnp.sum(weight * g_prob, -1, keepdims=True)
            g_score = (weight * (g_prob - inner)).astype(LOW)
            add_v = dot_tn(weight.astype(LOW), c_one)
            add_k = dot_tn(g_score, q_one)
            g_v = add_v if g_v is None else g_v + add_v
            g_k = add_k if g_k is None else g_k + add_k
            g_q.append(dot(g_score, key_pair))
        g_q = jnp.where(lead, g_q[0], g_q[1]) * HEAD_DIM**-0.5
        g_k = g_k * HEAD_DIM**-0.5
        gq_s[:, cut] = turn(g_q, cos_sel[...], -sin_sel[...]).astype(LOW)
        gk_s[:, cut] = turn(g_k, cos[...], -sin[...]).astype(LOW)
        gv_s[:, cut] = g_v.astype(LOW)
    rows = tok[...]
    spread(a_keep, a_send, 0, dw_out, dot_tn(tok_sel[...], gq_s[...]))
    spread(b_keep, b_send, 1, dot_tn(rows, gk_s[...]), dot_tn(rows, gv_s[...]))
    small_o[1:2, 0:local] = col_sum(gq_s[...].astype(F32))
    small_o[1:2, local : 2 * local] = col_sum(gk_s[...].astype(F32))
    small_o[1:2, 2 * local : 3 * local] = col_sum(gv_s[...].astype(F32))


def tokens_kernel(mpi, g_q, g_k, g_v, w_qkv, pos, g_pre, part_o):
    hot = one_hot(pos, g_k.shape[0]).astype(F32).astype(LOW)
    gq_full = dot_tn(hot, g_q[...]).astype(LOW)
    total = dot_nt(gq_full, w_qkv[0]) + dot_nt(g_k[...], w_qkv[1]) + dot_nt(g_v[...], w_qkv[2])
    part_o[...] = total

    @pl.when(mpi[0] == 0)
    def _():
        left = g_pre[...]
        spread = part_o[...]
        for _ in range(3):
            piece = left.astype(LOW)
            left = left - piece.astype(F32)
            spread = spread + dot_tn(hot, piece)
        part_o[...] = spread


def attend_kernel(query, keys, values, w_out, attn_o, ctx_s):
    pairs = query.shape[1] // PAIR
    for j in range(pairs):
        cut = slice(j * PAIR, (j + 1) * PAIR)
        q_pair = query[:, cut].astype(F32)
        lead = first_head(q_pair.shape)
        parts = []
        for side in range(2):
            chosen = jnp.where(lead if side == 0 else ~lead, q_pair, 0.0).astype(LOW)
            prob = softmax_of(dot_nt(chosen, keys[:, cut]) * HEAD_DIM**-0.5)
            parts.append(dot(prob.astype(LOW), values[:, cut]))
        ctx_s[:, cut] = jnp.where(lead, parts[0], parts[1]).astype(LOW)
    attn_o[...] = dot(ctx_s[...], w_out[...])


def feed_kernel(mine, other, tok, b_out, gain, shift, w_in, b_in, w_back, one_o, part_o):
    h_pre = tok[...].astype(F32) + (mine[...] + other[...] + b_out[...])
    hat, _ = center_of(h_pre)
    h_one = hat * gain[0:1, :] + shift[0:1, :]
    one_o[...] = h_one
    hidden = dot(h_one.astype(LOW), w_in[...]) + b_in[...]
    part_o[...] = dot((hidden * cdf_of(hidden)).astype(LOW), w_back[...])


def last_kernel(mine, other, h_one, b_back, gain, shift, out_o):
    z_sum = h_one[...] + (mine[...] + other[...] + b_back[...])
    hat, _ = center_of(z_sum)
    out_o[...] = (hat * gain[1:2, :] + shift[1:2, :]).astype(LOW)


def grads_kernel(
    h_one, grad_z, far_a, far_b, far_c, flipped, w_in, b_in, w_back, sel_in, sel_back,
    in_keep, in_send, back_keep, back_send,
):
    near, chunk = in_keep.shape[:2]
    part = far_a.shape[0] // 2
    fars = [far_a[...], far_b[...], far_c[...], flipped[...]]
    h_rows = [h_one[...]]
    g_rows = [grad_z[...]]
    for block in fars:
        for start in range(0, block.shape[0], 2 * part):
            h_rows.append(block[start : start + part])
            g_rows.append(block[start + part : start + 2 * part])
    h_low = jnp.concatenate(h_rows, 0).astype(LOW)
    g_low = jnp.concatenate(g_rows, 0).astype(LOW)
    hidden = dot(h_low, w_in[...]) + b_in[...]
    cdf = cdf_of(hidden)
    act = (hidden * cdf).astype(LOW)
    grad_u = (dot_nt(g_low, w_back[...]) * gelu_slope(hidden, cdf)).astype(LOW)
    h_cols = dot(h_low, sel_in[...]).astype(LOW)
    g_cols = dot(g_low, sel_back[...]).astype(LOW)
    d_in = dot_tn(h_cols, grad_u)
    d_back = dot_tn(g_cols, act)
    for c in range(near):
        in_keep[c] = d_in[c * chunk : (c + 1) * chunk]
        back_keep[c] = d_back[c * chunk : (c + 1) * chunk]
        in_send[c] = d_in[(near + c) * chunk : (near + c + 1) * chunk]
        back_send[c] = d_back[(near + c) * chunk : (near + c + 1) * chunk]


def finish_kernel(keep_a, got_a, keep_b, got_b, keep_in, got_in, keep_back, got_back, out_o, qkv_o, in_o, back_o):
    local = out_o.shape[1]
    out_o[...] = keep_a[0, :, :local] + got_a[0, :, :local]
    qkv_o[0] = keep_a[0, :, local:] + got_a[0, :, local:]
    qkv_o[1] = keep_b[0, :, :local] + got_b[0, :, :local]
    qkv_o[2] = keep_b[0, :, local:] + got_b[0, :, local:]
    in_o[...] = keep_in[0] + got_in[0]
    back_o[...] = keep_back[0] + got_back[0]


def call(kernel, outs, *args, scalars=0, scratch=()):
    specs = [pl.BlockSpec(memory_space=pltpu.SMEM)] * scalars
    specs += [pl.BlockSpec(memory_space=pltpu.VMEM)] * (len(args) - scalars)
    shapes = [jax.ShapeDtypeStruct(*item) for item in outs]
    result = pl.pallas_call(
        kernel,
        out_shape=shapes if len(shapes) > 1 else shapes[0],
        in_specs=specs,
        scratch_shapes=list(scratch),
    )
    return result(*args)


def shards(
    count,
    tokens,
    cotangent,
    masked_pos,
    w_qkv,
    b_qkv,
    w_out,
    b_out,
    w_in,
    b_in,
    w_back,
    b_back,
    ln_gain,
    ln_bias,
):
    _, length, width = tokens.shape
    local = w_qkv.shape[2]
    hidden = w_in.shape[1]
    slots = masked_pos.shape[1]
    heads = local // HEAD_DIM
    bits = count.bit_length() - 1
    chunk = width // count
    near = count // 4
    near_bits = bits - 2
    me = lax.axis_index("dp")
    core = lax.axis_index("mp").astype(jnp.int32)[None]
    cos, sin = tables(length)

    def flip(value):
        return lax.ppermute(value, "mp", [(0, 1), (1, 0)])

    def across(value, bit):
        return lax.ppermute(value, "dp", [(i, i ^ (1 << bit)) for i in range(count)])

    def halve(keep, send, order):
        for bit in order:
            got = across(send, bit)
            half = got.shape[0] // 2
            if half:
                send = keep[half:] + got[half:]
                keep = keep[:half] + got[:half]
        return keep, got

    def slot_of(index, order):
        total = jnp.zeros_like(index)
        for at, bit in enumerate(order):
            total = total + (((index >> bit) & 1) << (len(order) - 1 - at))
        return total

    z_low, z_high = bits - 2, bits - 1
    rest = list(range(2, near_bits))
    order_a = [0, 1] + rest + [z_low, z_high]
    order_b = [1, 0] + rest + [z_low, z_high]
    order_in = [0, 1] + rest
    order_back = [1, 0] + rest
    delta = jnp.arange(count, dtype=jnp.int32) ^ me.astype(jnp.int32)
    place = jnp.stack([slot_of(delta, o) for o in (order_a, order_b)])

    def columns(order):
        index = jnp.arange(width, dtype=jnp.int32)
        number = index // chunk
        spot = slot_of((number % near) ^ (me % near).astype(jnp.int32), order) * chunk + index % chunk
        spot = jnp.where(number // near == me // near, spot, -1)
        return (spot[:, None] == jnp.arange(near * chunk, dtype=jnp.int32)).astype(LOW)

    sel_in = columns(order_in)
    sel_back = columns(order_back)

    def gather_far(value):
        return [
            lax.ppermute(value, "dp", [(i, (i + step * near) % count) for i in range(count)])
            for step in (2, 1, 3)
        ]

    tok = tokens[0]
    cot = cotangent[0]
    pos = masked_pos.reshape(slots, 1)
    b_out, b_in, b_back = b_out[None], b_in[None], b_back[None]

    query, keys, values, q_sel, tok_sel, cos_sel, sin_sel, prob, ctx_sel, attn = call(
        front_kernel,
        [
            ((length, local), LOW),
            ((length, local), LOW),
            ((length, local), LOW),
            ((slots, local), LOW),
            ((slots, width), LOW),
            ((slots, PAIR), F32),
            ((slots, PAIR), F32),
            ((heads, slots, length), F32),
            ((slots, local), LOW),
            ((slots, width), F32),
        ],
        tok, w_qkv, b_qkv, cos, sin, pos, w_out,
    )
    h_one, part, hat, scale, slope = call(
        mid_kernel,
        [
            ((slots, width), F32),
            ((slots, width), F32),
            ((slots, width), F32),
            ((slots, 1), F32),
            ((slots, hidden), F32),
        ],
        attn, flip(attn), tok_sel, b_out, ln_gain, ln_bias, w_in, b_in, w_back,
    )
    grad_z, half_rows, part, small = call(
        turn_kernel,
        [
            ((slots, width), F32),
            ((slots, width), F32),
            ((slots, width), F32),
            ((8, hidden), F32),
        ],
        core, part, flip(part), h_one, b_back, ln_gain, cot, pos, slope, w_in, w_back,
        scalars=1,
    )
    grad_h_other = flip(part)
    far = gather_far(half_rows)
    far_flipped = flip(jnp.concatenate(far, 0))
    shape = ((count // 2, chunk, 2 * local), F32)
    a_keep, a_send, b_keep, b_send, g_q, g_k, g_v, small, g_pre = call(
        back_kernel,
        [
            shape,
            shape,
            shape,
            shape,
            ((slots, local), LOW),
            ((length, local), LOW),
            ((length, local), LOW),
            ((8, hidden), F32),
            ((slots, width), F32),
        ],
        place, part, grad_h_other, grad_z, hat, scale, ln_gain, tok, tok_sel, ctx_sel, w_out, q_sel, keys, values,
        prob, cos, sin, cos_sel, sin_sel, small,
        scalars=1,
    )
    back_part = call(tokens_kernel, [((length, width), F32)], core, g_q, g_k, g_v, w_qkv, pos, g_pre, scalars=1)
    shape = ((near // 2, chunk, hidden), F32)
    in_keep, in_send, back_keep, back_send = call(
        grads_kernel, [shape] * 4, h_one, grad_z, *far, far_flipped, w_in, b_in, w_back, sel_in, sel_back
    )
    query, g_pre = lax.optimization_barrier((query, g_pre))
    attn = call(
        attend_kernel, [((length, width), F32)], query, keys, values, w_out,
        scratch=[pltpu.VMEM((length, local), LOW)],
    )
    h_full, part = call(
        feed_kernel,
        [((length, width), F32), ((length, width), F32)],
        attn, flip(attn), tok, b_out, ln_gain, ln_bias, w_in, b_in, w_back,
    )
    output = call(
        last_kernel, [((length, width), LOW)], part, flip(part), h_full, b_back, ln_gain, ln_bias
    )
    grad_tokens = jnp.add(back_part, flip(back_part))
    for bit in range(bits - 1):
        small = small + across(small, bit)
    small_got = across(small, bits - 1)
    last_a = halve(a_keep, a_send, order_a)
    last_b = halve(b_keep, b_send, order_b)
    last_in = halve(in_keep, in_send, order_in)
    last_back = halve(back_keep, back_send, order_back)
    small, keep_in, keep_back = lax.optimization_barrier((small, last_in[0], last_back[0]))
    small = small + small_got
    last_in, last_back = (keep_in, last_in[1]), (keep_back, last_back[1])
    sum_out, sum_qkv, sum_in, sum_back = call(
        finish_kernel,
        [((chunk, local), F32), ((3, chunk, local), F32), ((chunk, hidden), F32), ((chunk, hidden), F32)],
        *last_a, *last_b, *last_in, *last_back,
    )
    return (
        output[None],
        grad_tokens[None],
        sum_qkv,
        small[1, : 3 * local].reshape(3, local),
        sum_out.T,
        small[2, :width],
        sum_in,
        small[0],
        sum_back.T,
        small[2, width:],
        small[3].reshape(2, width),
        small[4].reshape(2, width),
    )


def solution(mesh):
    in_specs = (
        P("dp", None, None),
        P("dp", None, None),
        P("dp", None),
        P(None, None, "mp"),
        P(None, "mp"),
        P("mp", None),
        P(),
        P(None, "mp"),
        P("mp"),
        P("mp", None),
        P(),
        P(),
        P(),
    )
    out_specs = (
        P("dp", None, None),
        P("dp", None, None),
        P(None, "dp", "mp"),
        P(None, "mp"),
        P("mp", "dp"),
        P(),
        P("dp", "mp"),
        P("mp"),
        P("mp", "dp"),
        P(),
        P(),
        P(),
    )
    count = mesh.shape["dp"]

    def body(*args):
        return shards(count, *args)

    return jax.shard_map(body, mesh=mesh, in_specs=in_specs, out_specs=out_specs, check_vma=False)
```
